32 devices in a mesh: fsdp: 16 (over z, y, x), dp: 2 (over core).
Axes of the slice: x: 2, y: 2, z: 4, core: 2. Of those that a mesh axis runs over, the one named last changes fastest.
Arguments:
- grad_parts: bfloat16 [2, 16, 512, 512], P('dp', None, 'fsdp'), may hold values from -2.5 to 2.5
- weights: float32 [16, 512, 512], P(None, 'fsdp', 'dp'), may hold values from -6 to 6
- left_stat: float32 [48, 512, 512], P('fsdp', 'dp'), may hold values from -6 to 6
- right_stat: float32 [48, 512, 512], P('fsdp', 'dp'), may hold values from -6 to 6
- left_codes: bfloat16 [48, 512, 512], P('fsdp'), may hold values from -1 to 1
- right_codes: bfloat16 [48, 512, 512], P('fsdp', 'dp'), may hold values from -1 to 1
- left_scales: float32 [48, 512], P('fsdp'), may hold values from 0.3 to 3
- right_scales: float32 [48, 512], P('fsdp', 'dp'), may hold values from 0.1 to 27
- owners: int32 [16], replicated, may hold values from 0 to 15, as said below
Outputs:
- new_weights: float32 [16, 512, 512], P(None, 'fsdp', 'dp')
- new_left_stat: float32 [48, 512, 512], P('fsdp', 'dp')
- new_right_stat: float32 [48, 512, 512], P('fsdp', 'dp')
The draws below stay inside these ranges and needn't reach their ends.
Inputs may be any that keep to these rules, and one draw needn't show every extreme that they name: `owners`: each owner is named by at most 3 blocks, and some owner by exactly 3 blocks.
All inputs are finite; a program needn't handle non-finite values.
Results may differ from the reference program's by a relative error of at most 0.0095.
Values may be sent and summed in bfloat16 or wider, within the bound.
A program may use at most 64 MiB of HBM per device.

```python
import math
import jax
import jax.numpy as jnp
from jax import lax

B = 512
MOST = 3
NB = 16
SLOTS = 48
N_DP = 2


def draw_owners(key, part):
    first_key, second_key, third_key = jax.random.split(jax.random.fold_in(key, 7), 3)
    shuffle = jax.random.permutation(first_key, NB).astype(jnp.int32)
    heavy_count = jax.random.randint(second_key, (), 1, NB // (2 * MOST) + 1)
    positions = jnp.arange(NB, dtype=jnp.int32)
    counts = jnp.where(positions < heavy_count, MOST, jnp.where(positions < MOST * heavy_count, 0, 1)).astype(jnp.int32)
    bounds = jnp.cumsum(counts)
    picked = jnp.sum((bounds[None, :] <= positions[:, None]).astype(jnp.int32), axis=1)
    ordered = shuffle[picked]
    return ordered[jax.random.permutation(third_key, NB)].astype(jnp.int32)


def draw_right_scales(key, part):
    scale_key = jax.random.fold_in(key, 11)
    row_frac = jnp.arange(B, dtype=jnp.float32) / (B - 1)
    bottom = jnp.log(0.3)
    growth = jnp.log(3.0)
    uniform_log = jax.random.uniform(scale_key, (SLOTS, B), jnp.float32, bottom, jnp.log(3.0))
    return jnp.exp(uniform_log + growth * row_frac[None, :]).astype(jnp.float32)


def shard_levels(own_key, extent, cuts, smallest, high):
    gain, own = 1.0, jax.random.fold_in(own_key, 6)
    for axis_at, parts in cuts:
        steps = jnp.exp(jax.random.uniform(jax.random.fold_in(own, axis_at), (parts,), jnp.float32, smallest / len(cuts), high / len(cuts)))
        gain = gain * jnp.repeat(steps, extent[axis_at] // parts).reshape([-1 if axis == axis_at else 1 for axis in range(len(extent))])
    return gain


def scatter_about(key, shape, spread, limit, cuts=(), kind=jnp.bfloat16):
    drawn = spread * jax.random.normal(key, shape, jnp.float32)
    if cuts:
        drawn = drawn * shard_levels(key, shape, cuts, -0.22, 0.18)
    return jnp.clip(drawn, -limit, limit).astype(kind)


def setup_inputs(seed: int = 0) -> dict:
    streams_of = jax.random.split(jax.random.key(seed), 10)
    grad_parts = scatter_about(streams_of[0], (N_DP, NB, B, B), 0.35, 2.5, ((0, 2), (2, 16)))
    weights = scatter_about(streams_of[1], (NB, B, B), 1.0, 6.0, ((1, 16), (2, 2)), jnp.float32)
    left_stat = scatter_about(streams_of[2], (SLOTS, B, B), 1.0, 6.0, ((0, 16), (1, 2)), jnp.float32)
    right_stat = scatter_about(streams_of[3], (SLOTS, B, B), 1.0, 6.0, ((0, 16), (1, 2)), jnp.float32)
    left_codes = jnp.clip(jax.random.uniform(streams_of[4], (SLOTS, B, B), jnp.float32, -1.0, 1.0) * shard_levels(streams_of[4], (SLOTS, B, B), ((0, 16),), -0.4, 0.0), -1.0, 1.0).astype(jnp.bfloat16)
    right_codes = jnp.clip(jax.random.uniform(streams_of[5], (SLOTS, B, B), jnp.float32, -1.0, 1.0) * shard_levels(streams_of[5], (SLOTS, B, B), ((0, 16), (1, 2)), -0.4, 0.0), -1.0, 1.0).astype(jnp.bfloat16)
    left_scales = jnp.clip(jnp.exp(math.log(3.0) - 2.3025851 * jax.random.uniform(streams_of[6], (SLOTS, B), jnp.float32) ** shard_levels(streams_of[6], (SLOTS, B), ((0, 16),), -0.2, 0.2)), 0.3, 3.0)
    right_scales = draw_right_scales(jax.random.fold_in(streams_of[9], 71), 0)
    owners = draw_owners(jax.random.fold_in(streams_of[9], 71), 0)
    return {"grad_parts": grad_parts, "weights": weights, "left_stat": left_stat, "right_stat": right_stat, "left_codes": left_codes, "right_codes": right_codes, "left_scales": left_scales, "right_scales": right_scales, "owners": owners}


stat_decay = 0.95
step_size = 0.5
epsilon = 1e-06

def slot_table(owners, capacity):
    count = owners.shape[0]
    index = jnp.arange(count, dtype=jnp.int32)
    earlier = (owners[:, None] == owners[None, :]) & (index[None, :] < index[:, None])
    rank = lax.optimization_barrier(jnp.sum(earlier.astype(jnp.int32), axis=1)).astype(jnp.int32)
    return (owners * capacity + rank).astype(jnp.int32)

def reference(grad_parts, weights, left_stat, right_stat, left_codes, right_codes, left_scales, right_scales, owners):
    grad = lax.optimization_barrier(jnp.sum(grad_parts.astype(jnp.float32), axis=0)).astype(jnp.bfloat16)
    slot_of = slot_table(owners, MOST)
    slot_ids = jnp.arange(SLOTS, dtype=jnp.int32)
    matches = slot_of[None, :] == slot_ids[:, None]
    block_ids = jnp.arange(NB, dtype=jnp.int32)
    source = lax.optimization_barrier(jnp.sum(jnp.where(matches, block_ids[None, :], 0), axis=1)).astype(jnp.int32)
    filled = jnp.any(matches, axis=1)

    def per_slot(slot_index):
        taken = lax.dynamic_index_in_dim(grad, source[slot_index], 0, keepdims=False)
        block_grad = jnp.where(filled[slot_index], taken, jnp.zeros_like(taken))
        gram_left = jnp.dot(block_grad, block_grad.T, preferred_element_type=jnp.float32)
        gram_right = jnp.dot(block_grad.T, block_grad, preferred_element_type=jnp.float32)
        left_new = stat_decay * left_stat[slot_index] + (1.0 - stat_decay) * gram_left
        right_new = stat_decay * right_stat[slot_index] + (1.0 - stat_decay) * gram_right
        left_factor = (left_codes[slot_index].astype(jnp.float32) * left_scales[slot_index][:, None]).astype(jnp.bfloat16)
        right_factor = (right_codes[slot_index].astype(jnp.float32) * right_scales[slot_index][:, None]).astype(jnp.bfloat16)
        mixed = jnp.dot(block_grad, right_factor.T, preferred_element_type=jnp.float32).astype(jnp.bfloat16)
        precond = jnp.dot(left_factor, mixed, preferred_element_type=jnp.float32)
        grad_squares = jnp.sum(jnp.square(block_grad.astype(jnp.float32)))
        pre_squares = jnp.sum(precond * precond)
        graft_ratio = jnp.sqrt(grad_squares) * lax.rsqrt(pre_squares + epsilon)
        return (left_new, right_new, step_size * graft_ratio * precond)
    left_new, right_new, updates = lax.map(per_slot, slot_ids)
    new_weights = weights - jnp.take(updates, slot_of, axis=0)
    return (new_weights, left_new, right_new)
```

```python
import functools

import jax
import jax.numpy as jnp
from jax import lax
from jax.experimental import pallas as pl
from jax.experimental.pallas import tpu as pltpu
from jax.sharding import PartitionSpec as P

stat_decay = 0.95
step_size = 0.5
epsilon = 1e-06
MESH = pl.DeviceIdType.MESH


def slot_table(owners, capacity):
    count = owners.shape[0]
    index = jnp.arange(count, dtype=jnp.int32)
    earlier = (owners[:, None] == owners[None, :]) & (index[None, :] < index[:, None])
    rank = jnp.sum(earlier.astype(jnp.int32), axis=1)
    return owners * capacity + rank


def greet(n, me, core):
    barrier = pltpu.get_barrier_semaphore()

    @pl.loop(1, n)
    def _(k):
        peer = lax.rem(me + k, n)
        pl.semaphore_signal(barrier, inc=1, device_id=(peer, core), device_id_type=MESH)

    pl.semaphore_signal(barrier, inc=1, device_id=(me, 1 - core), device_id_type=MESH)
    pl.semaphore_wait(barrier, n)


def scatter_kernel(
    n, cap, source_ref, grad_ref, whole, theirs, summed, stage,
    swap_send, swap_recv, out_send, out_recv, fwd_send, fwd_recv, own_sem,
):
    me = lax.axis_index("fsdp")
    core = lax.axis_index("dp")
    blocks, rows, _ = grad_ref.shape
    half = rows // 2
    greet(n, me, core)

    other_rows = pl.ds(pl.multiple_of((1 - core) * half, half), half)
    my_rows = pl.ds(pl.multiple_of(core * half, half), half)
    swap = pltpu.make_async_remote_copy(
        src_ref=grad_ref.at[:, other_rows, :], dst_ref=theirs,
        send_sem=swap_send, recv_sem=swap_recv,
        device_id=(me, 1 - core), device_id_type=MESH,
    )
    swap.start()
    swap.wait()
    summed[...] = (
        grad_ref[:, my_rows, :].astype(jnp.float32) + theirs[...].astype(jnp.float32)
    ).astype(jnp.bfloat16)

    @pl.loop(0, n * cap)
    def _(j):
        code = source_ref[j]
        piece = summed[lax.max(code, 0)].astype(jnp.float32)
        keep = jnp.where(code >= 0, 1.0, 0.0).astype(jnp.float32)
        stage[j] = (piece * keep).astype(jnp.bfloat16)

    def landing(device, its_core):
        start = pl.multiple_of(device * rows + its_core * half, half)
        return whole.at[:, pl.ds(start, half), :]

    def outgoing(k):
        peer = lax.rem(me + k, n)
        return pltpu.make_async_remote_copy(
            src_ref=stage.at[pl.ds(peer * cap, cap)], dst_ref=landing(me, core),
            send_sem=out_send.at[k], recv_sem=out_recv.at[k],
            device_id=(peer, core), device_id_type=MESH,
        )

    def incoming(k):
        peer = lax.rem(me - k + n, n)
        return pltpu.make_async_remote_copy(
            src_ref=stage.at[pl.ds(peer * cap, cap)], dst_ref=landing(peer, core),
            send_sem=out_send.at[k], recv_sem=out_recv.at[k],
            device_id=(peer, core), device_id_type=MESH,
        )

    def forward(k, its_core):
        peer = lax.rem(me - k + n, n)
        return pltpu.make_async_remote_copy(
            src_ref=landing(peer, its_core), dst_ref=landing(peer, its_core),
            send_sem=fwd_send.at[k], recv_sem=fwd_recv.at[k],
            device_id=(me, 1 - core), device_id_type=MESH,
        )

    @pl.loop(1, n)
    def _(k):
        outgoing(k).start()

    own = pltpu.make_async_copy(stage.at[pl.ds(me * cap, cap)], landing(me, core), own_sem)
    own.start()
    own.wait()
    forward(0, core).start()

    @pl.loop(1, n)
    def _(k):
        incoming(k).wait_recv()
        forward(k, core).start()

    @pl.loop(1, n)
    def _(k):
        outgoing(k).wait_send()

    @pl.loop(0, n)
    def _(k):
        forward(k, core).wait_send()
        forward(k, 1 - core).wait_recv()


def return_kernel(
    n, cap, place_ref, scale_row_ref, pre_ref, squares_ref, weights_ref, out_ref,
    landed, other_squares, graft, grafts,
    swap_send, swap_recv, out_send, out_recv, tiny_send, tiny_recv,
):
    me = lax.axis_index("fsdp")
    core = lax.axis_index("dp")
    blocks, rows, _ = weights_ref.shape
    greet(n, me, core)

    def transfer(k, peer, source):
        return pltpu.make_async_remote_copy(
            src_ref=pre_ref.at[:, pl.ds(pl.multiple_of(peer * rows, rows), rows), :],
            dst_ref=landed.at[pl.ds(source * cap, cap)],
            send_sem=out_send.at[k], recv_sem=out_recv.at[k],
            device_id=(peer, core), device_id_type=MESH,
        )

    def tiny(k, peer, source):
        return pltpu.make_async_remote_copy(
            src_ref=graft, dst_ref=grafts.at[source],
            send_sem=tiny_send.at[k], recv_sem=tiny_recv.at[k],
            device_id=(peer, core), device_id_type=MESH,
        )

    swap = pltpu.make_async_remote_copy(
        src_ref=squares_ref, dst_ref=other_squares,
        send_sem=swap_send, recv_sem=swap_recv,
        device_id=(me, 1 - core), device_id_type=MESH,
    )
    swap.start()

    @pl.loop(1, n)
    def _(k):
        transfer(k, lax.rem(me + k, n), me).start()

    landed[pl.ds(me * cap, cap)] = pre_ref[
        :, pl.ds(pl.multiple_of(me * rows, rows), rows), :
    ]
    swap.wait()
    total = squares_ref[0] + other_squares[0]
    scale = step_size * jnp.sqrt(squares_ref[1]) * lax.rsqrt(total + epsilon)
    graft[...] = scale
    grafts[me] = scale

    @pl.loop(1, n)
    def _(k):
        tiny(k, lax.rem(me + k, n), me).start()

    @pl.loop(1, n)
    def _(k):
        peer = lax.rem(me - k + n, n)
        transfer(k, peer, peer).wait_recv()
        tiny(k, peer, peer).wait_recv()

    @pl.loop(0, blocks)
    def _(b):
        slot = place_ref[b]
        factor = grafts[scale_row_ref[b]]
        rank = lax.rem(slot, cap)
        picked = jnp.where(
            lax.broadcasted_iota(jnp.int32, factor.shape, 0) == rank, factor, 0.0
        )
        amount = jnp.sum(picked[:, 0:1])
        out_ref[b] = weights_ref[b] - amount * landed[slot].astype(jnp.float32)

    @pl.loop(1, n)
    def _(k):
        transfer(k, lax.rem(me + k, n), me).wait_send()
        tiny(k, lax.rem(me + k, n), me).wait_send()


def kernels_fit(rows, width):
    return lax.axis_size("dp") == 2 and rows % 32 == 0 and width % 128 == 0


def fast(
    grad_parts, weights, left_stat, right_stat, left_codes, right_codes,
    left_scales, right_scales, owners,
):
    n = lax.axis_size("fsdp")
    replica = lax.axis_index("dp")
    cap, width, size = left_stat.shape
    blocks, rows = weights.shape[:2]
    half = rows // 2
    slot_of = slot_table(owners, cap)
    slot_ids = jnp.arange(n * cap, dtype=jnp.int32)
    matches = slot_of[None, :] == slot_ids[:, None]
    block_ids = jnp.arange(blocks, dtype=jnp.int32)
    source = jnp.sum(jnp.where(matches, block_ids[None, :] + 1, 0), axis=1) - 1

    vmem = pl.BlockSpec(memory_space=pltpu.VMEM)
    smem = pl.BlockSpec(memory_space=pltpu.SMEM)
    dma = pltpu.SemaphoreType.DMA
    whole_grad = pl.pallas_call(
        functools.partial(scatter_kernel, n, cap),
        out_shape=jax.ShapeDtypeStruct((cap, size, size), jnp.bfloat16),
        in_specs=[smem, vmem],
        out_specs=vmem,
        scratch_shapes=[
            pltpu.VMEM((blocks, half, size), jnp.bfloat16),
            pltpu.VMEM((blocks, half, size), jnp.bfloat16),
            pltpu.VMEM((n * cap, half, size), jnp.bfloat16),
            dma, dma, dma((n,)), dma((n,)), dma((n,)), dma((n,)), dma,
        ],
        compiler_params=pltpu.CompilerParams(collective_id=0, has_side_effects=True),
    )(source, grad_parts[0])

    left_factor = (left_codes.astype(jnp.float32) * left_scales[:, :, None]).astype(jnp.bfloat16)
    right_factor = (right_codes.astype(jnp.float32) * right_scales[:, :, None]).astype(jnp.bfloat16)
    mixed = jnp.einsum(
        "sik,sck->sic", whole_grad, right_factor, preferred_element_type=jnp.float32
    ).astype(jnp.bfloat16)
    precond = jnp.einsum("sik,skc->sic", left_factor, mixed, preferred_element_type=jnp.float32)
    part_squares = jnp.sum(precond * precond, axis=(1, 2))
    grad_squares = jnp.sum(jnp.square(whole_grad.astype(jnp.float32)), axis=(1, 2))
    squares = jnp.stack([part_squares, grad_squares])
    squares = jnp.pad(squares, ((0, 0), (0, (-cap) % 8)))
    squares = jnp.broadcast_to(squares[:, :, None], squares.shape + (128,))

    lanes = squares.shape[1:]
    new_weights = pl.pallas_call(
        functools.partial(return_kernel, n, cap),
        out_shape=jax.ShapeDtypeStruct(weights.shape, jnp.float32),
        in_specs=[smem, smem, vmem, vmem, vmem],
        out_specs=vmem,
        scratch_shapes=[
            pltpu.VMEM((n * cap, rows, width), jnp.bfloat16),
            pltpu.VMEM(squares.shape, jnp.float32),
            pltpu.VMEM(lanes, jnp.float32),
            pltpu.VMEM((n,) + lanes, jnp.float32),
            dma, dma, dma((n,)), dma((n,)), dma((n,)), dma((n,)),
        ],
        compiler_params=pltpu.CompilerParams(collective_id=1, has_side_effects=True),
    )(slot_of, owners, precond.astype(jnp.bfloat16), squares, weights)

    first_row = replica * width
    rows_mine = lax.dynamic_slice_in_dim(whole_grad, first_row, width, 1)
    cols_mine = lax.dynamic_slice_in_dim(whole_grad, first_row, width, 2)
    gram_left = jnp.einsum("srk,sck->src", rows_mine, whole_grad, preferred_element_type=jnp.float32)
    gram_right = jnp.einsum("skr,skc->src", cols_mine, whole_grad, preferred_element_type=jnp.float32)
    left_new = stat_decay * left_stat + (1.0 - stat_decay) * gram_left
    right_new = stat_decay * right_stat + (1.0 - stat_decay) * gram_right
    return (new_weights, left_new, right_new)


def route_rows(summed, picker, owner_count, capacity):
    blocks = summed.shape[0]
    flat = summed.reshape(blocks, -1)
    placed = jnp.einsum("bj,bx->jx", picker, flat, preferred_element_type=jnp.float32).astype(
        jnp.bfloat16
    )
    return placed.reshape(owner_count, capacity, summed.shape[1], summed.shape[2])


def local(
    grad_parts, weights, left_stat, right_stat, left_codes, right_codes,
    left_scales, right_scales, owners,
):
    if kernels_fit(weights.shape[1], left_stat.shape[1]):
        return fast(
            grad_parts, weights, left_stat, right_stat, left_codes, right_codes,
            left_scales, right_scales, owners,
        )
    owner_count = lax.axis_size("fsdp")
    replica = lax.axis_index("dp")
    capacity = left_stat.shape[0]
    piece_width = left_stat.shape[1]
    block_width = left_codes.shape[1]
    slot_of = slot_table(owners, capacity)
    slot_ids = jnp.arange(owner_count * capacity, dtype=jnp.int32)
    picker = (slot_of[:, None] == slot_ids[None, :]).astype(jnp.bfloat16)
    partial_value = grad_parts[0].astype(jnp.float32)
    summed = lax.psum_scatter(
        partial_value.astype(jnp.bfloat16), "dp", scatter_dimension=2, tiled=True
    )
    routed = route_rows(summed, picker, owner_count, capacity)
    arrived = lax.all_to_all(routed, "fsdp", split_axis=0, concat_axis=2, tiled=True)
    column_part = arrived.reshape(capacity, block_width, piece_width)
    whole_grad = lax.all_gather(column_part, "dp", axis=2, tiled=True)
    first_row = replica * piece_width
    rows_mine = lax.dynamic_slice_in_dim(whole_grad, first_row, piece_width, 1)
    cols_mine = lax.dynamic_slice_in_dim(whole_grad, first_row, piece_width, 2)
    gram_left = jnp.einsum(
        "srk,sck->src", rows_mine, whole_grad, preferred_element_type=jnp.float32
    )
    gram_right = jnp.einsum(
        "skr,skc->src", cols_mine, whole_grad, preferred_element_type=jnp.float32
    )
    left_new = stat_decay * left_stat + (1.0 - stat_decay) * gram_left
    right_new = stat_decay * right_stat + (1.0 - stat_decay) * gram_right
    left_factor = (left_codes.astype(jnp.float32) * left_scales[:, :, None]).astype(jnp.bfloat16)
    right_factor = (right_codes.astype(jnp.float32) * right_scales[:, :, None]).astype(jnp.bfloat16)
    mixed = jnp.einsum(
        "sik,sck->sic", whole_grad, right_factor, preferred_element_type=jnp.float32
    ).astype(jnp.bfloat16)
    precond = jnp.einsum("sik,skc->sic", left_factor, mixed, preferred_element_type=jnp.float32)
    part_squares = jnp.sum(precond * precond, axis=(1, 2))
    total_squares = lax.psum(part_squares, "dp")
    grad_squares = jnp.sum(jnp.square(whole_grad.astype(jnp.float32)), axis=(1, 2))
    graft_ratio = jnp.sqrt(grad_squares) * lax.rsqrt(total_squares + epsilon)
    update = step_size * graft_ratio[:, None, None] * precond
    returned = lax.all_to_all(update, "fsdp", split_axis=1, concat_axis=0, tiled=True)
    my_update = jnp.take(returned, slot_of, axis=0)
    new_weights = weights - my_update
    return (new_weights, left_new, right_new)


def solution(mesh):
    return jax.shard_map(
        local,
        mesh=mesh,
        in_specs=(
            P("dp", None, "fsdp", None),
            P(None, "fsdp", "dp"),
            P("fsdp", "dp", None),
            P("fsdp", "dp", None),
            P("fsdp", None, None),
            P("fsdp", "dp", None),
            P("fsdp", None),
            P("fsdp", "dp"),
            P(),
        ),
        out_specs=(P(None, "fsdp", "dp"), P("fsdp", "dp", None), P("fsdp", "dp", None)),
        check_vma=False,
    )
```

```python
import functools

import jax
import jax.numpy as jnp
from jax import lax
from jax.experimental import pallas as pl
from jax.experimental.pallas import tpu as pltpu
from jax.sharding import PartitionSpec as P

stat_decay = 0.95
step_size = 0.5
epsilon = 1e-06
MESH = pl.DeviceIdType.MESH


def slot_table(owners, capacity):
    count = owners.shape[0]
    index = jnp.arange(count, dtype=jnp.int32)
    earlier = (owners[:, None] == owners[None, :]) & (index[None, :] < index[:, None])
    rank = jnp.sum(earlier.astype(jnp.int32), axis=1)
    return owners * capacity + rank


def greet(n, me, core):
    barrier = pltpu.get_barrier_semaphore()

    @pl.loop(1, n)
    def _(k):
        peer = lax.rem(me + k, n)
        pl.semaphore_signal(barrier, inc=1, device_id=(peer, core), device_id_type=MESH)

    pl.semaphore_signal(barrier, inc=1, device_id=(me, 1 - core), device_id_type=MESH)
    pl.semaphore_wait(barrier, n)


def step_kernel(
    n, cap, source_ref, slot_ref, owner_ref, rank_ref,
    grad_ref, left_scale_ref, right_scale_ref, left_hbm, right_hbm, weights_hbm,
    whole, out_ref,
    theirs, summed, stage, left_ref, right_ref, weights_ref, mixed_ref, pre_ref, landed,
    squares, other_squares, graft, grafts,
    load_sem, swap_send, swap_recv, own_sem, out_send, out_recv, fwd_send, fwd_recv,
    back_send, back_recv, sq_send, sq_recv, tiny_send, tiny_recv,
):
    me = lax.axis_index("fsdp")
    core = lax.axis_index("dp")
    blocks, rows, size = grad_ref.shape
    half = rows // 2
    loads = [
        pltpu.make_async_copy(right_hbm, right_ref, load_sem.at[0]),
        pltpu.make_async_copy(left_hbm, left_ref, load_sem.at[1]),
        pltpu.make_async_copy(weights_hbm, weights_ref, load_sem.at[2]),
    ]
    for load in loads:
        load.start()
    greet(n, me, core)

    other_rows = pl.ds(pl.multiple_of((1 - core) * half, half), half)
    my_rows = pl.ds(pl.multiple_of(core * half, half), half)
    swap = pltpu.make_async_remote_copy(
        src_ref=grad_ref.at[:, other_rows, :], dst_ref=theirs,
        send_sem=swap_send, recv_sem=swap_recv,
        device_id=(me, 1 - core), device_id_type=MESH,
    )
    swap.start()
    swap.wait()
    summed[...] = (
        grad_ref[:, my_rows, :].astype(jnp.float32) + theirs[...].astype(jnp.float32)
    ).astype(jnp.bfloat16)

    def landing(slot, device, its_core):
        start = pl.multiple_of(device * rows + its_core * half, half)
        return whole.at[slot, pl.ds(start, half), :]

    def outward(slot, k, peer, origin):
        return pltpu.make_async_remote_copy(
            src_ref=stage.at[slot, peer], dst_ref=landing(slot, origin, core),
            send_sem=out_send.at[slot, k], recv_sem=out_recv.at[slot, k],
            device_id=(peer, core), device_id_type=MESH,
        )

    def forward(slot, k, its_core):
        peer = lax.rem(me - k + n, n)
        return pltpu.make_async_remote_copy(
            src_ref=landing(slot, peer, its_core), dst_ref=landing(slot, peer, its_core),
            send_sem=fwd_send.at[slot, k], recv_sem=fwd_recv.at[slot, k],
            device_id=(me, 1 - core), device_id_type=MESH,
        )

    def back(slot, k, peer, origin):
        return pltpu.make_async_remote_copy(
            src_ref=pre_ref.at[slot, pl.ds(pl.multiple_of(peer * rows, rows), rows), :],
            dst_ref=landed.at[origin * cap + slot],
            send_sem=back_send.at[slot, k], recv_sem=back_recv.at[slot, k],
            device_id=(peer, core), device_id_type=MESH,
        )

    def tiny(k, peer, origin):
        return pltpu.make_async_remote_copy(
            src_ref=graft, dst_ref=grafts.at[origin],
            send_sem=tiny_send.at[k], recv_sem=tiny_recv.at[k],
            device_id=(peer, core), device_id_type=MESH,
        )

    def swap_squares(slot):
        return pltpu.make_async_remote_copy(
            src_ref=squares.at[slot], dst_ref=other_squares.at[slot],
            send_sem=sq_send.at[slot], recv_sem=sq_recv.at[slot],
            device_id=(me, 1 - core), device_id_type=MESH,
        )

    def own(slot):
        return pltpu.make_async_copy(stage.at[slot, me], landing(slot, me, core), own_sem.at[slot])

    far = n // 2 - 2

    def nth(i):
        return 1 + lax.rem(i + far, n - 1)

    @pl.loop(0, cap)
    def _(slot):
        @pl.loop(0, n)
        def _(peer):
            code = source_ref[peer * cap + slot]
            piece = summed[lax.max(code, 0)].astype(jnp.float32)
            keep = jnp.where(code >= 0, 1.0, 0.0).astype(jnp.float32)
            stage[slot, peer] = (piece * keep).astype(jnp.bfloat16)

        own(slot).start()

        @pl.loop(0, n - 1)
        def _(i):
            k = nth(i)
            outward(slot, k, lax.rem(me + k, n), me).start()

    @pl.loop(0, cap)
    def _(slot):
        own(slot).wait()
        forward(slot, 0, core).start()

    for load in loads:
        load.wait()

    def scaled(codes, scale_row):
        count = codes.shape[0]
        column = jnp.transpose(jnp.broadcast_to(scale_row, (8, count)))[:, 0:1]
        return (codes.astype(jnp.float32) * column).astype(jnp.bfloat16)

    for slot in range(cap):
        right_ref[slot] = scaled(right_ref[slot], right_scale_ref[pl.ds(slot, 1), :])
        left_ref[slot] = scaled(left_ref[slot], left_scale_ref[pl.ds(slot, 1), :])

    @pl.loop(0, cap)
    def _(slot):
        @pl.loop(0, n - 1)
        def _(i):
            k = nth(i)
            outward(slot, k, me, lax.rem(me - k + n, n)).wait_recv()
            forward(slot, k, core).start()

        @pl.loop(0, n)
        def _(k):
            forward(slot, k, 1 - core).wait_recv()

        mixed_ref[...] = lax.dot_general(
            whole[slot], right_ref[slot], (((1,), (1,)), ((), ())),
            preferred_element_type=jnp.float32,
        ).astype(jnp.bfloat16)
        pre = jnp.dot(left_ref[slot], mixed_ref[...], preferred_element_type=jnp.float32)
        pre_ref[slot] = pre.astype(jnp.bfloat16)
        squares[slot] = jnp.full(squares.shape[1:], jnp.sum(pre * pre), jnp.float32)

        @pl.loop(0, n - 1)
        def _(i):
            k = nth(i)
            back(slot, k, lax.rem(me + k, n), me).start()

        swap_squares(slot).start()
        landed[me * cap + slot] = pre_ref[slot, pl.ds(pl.multiple_of(me * rows, rows), rows), :]

    line = lax.broadcasted_iota(jnp.int32, graft.shape, 0)
    factor = jnp.zeros(graft.shape, jnp.float32)
    for slot in range(cap):
        energy = jnp.sum(jnp.square(whole[slot].astype(jnp.float32)))
        swap_squares(slot).wait()
        total = squares[slot] + other_squares[slot]
        ratio = step_size * jnp.sqrt(jnp.full(graft.shape, energy, jnp.float32))
        factor = jnp.where(line == slot, ratio * lax.rsqrt(total + epsilon), factor)
    graft[...] = factor
    grafts[me] = factor

    @pl.loop(0, n - 1)
    def _(i):
        k = nth(i)
        tiny(k, lax.rem(me + k, n), me).start()

    @pl.loop(0, cap)
    def _(slot):
        @pl.loop(1, n)
        def _(k):
            back(slot, k, me, lax.rem(me - k + n, n)).wait_recv()

    @pl.loop(1, n)
    def _(k):
        tiny(k, me, lax.rem(me - k + n, n)).wait_recv()

    @pl.loop(0, blocks)
    def _(b):
        amount = grafts[owner_ref[b], pl.ds(rank_ref[b], 1), :]
        update = landed[slot_ref[b]].astype(jnp.float32)
        for start in range(0, update.shape[1], 128):
            part = slice(start, start + 128)
            out_ref[b, :, part] = weights_ref[b, :, part] - amount * update[:, part]

    @pl.loop(0, cap)
    def _(slot):
        @pl.loop(1, n)
        def _(k):
            peer = lax.rem(me + k, n)
            outward(slot, k, peer, me).wait_send()
            back(slot, k, peer, me).wait_send()

        @pl.loop(0, n)
        def _(k):
            forward(slot, k, core).wait_send()

    @pl.loop(1, n)
    def _(k):
        tiny(k, lax.rem(me + k, n), me).wait_send()


def kernels_fit(rows, width, capacity):
    return lax.axis_size("dp") == 2 and rows % 32 == 0 and width % 128 == 0 and capacity <= 8


def fast(
    grad_parts, weights, left_stat, right_stat, left_codes, right_codes,
    left_scales, right_scales, owners,
):
    n = lax.axis_size("fsdp")
    replica = lax.axis_index("dp")
    cap, width, size = left_stat.shape
    blocks, rows = weights.shape[:2]
    half = rows // 2
    slot_of = slot_table(owners, cap)
    slot_ids = jnp.arange(n * cap, dtype=jnp.int32)
    matches = slot_of[None, :] == slot_ids[:, None]
    block_ids = jnp.arange(blocks, dtype=jnp.int32)
    source = jnp.sum(jnp.where(matches, block_ids[None, :] + 1, 0), axis=1) - 1

    vmem = pl.BlockSpec(memory_space=pltpu.VMEM)
    smem = pl.BlockSpec(memory_space=pltpu.SMEM)
    hbm = pl.BlockSpec(memory_space=pl.ANY)
    dma = pltpu.SemaphoreType.DMA
    bf16, f32 = jnp.bfloat16, jnp.float32
    whole_grad, new_weights = pl.pallas_call(
        functools.partial(step_kernel, n, cap),
        out_shape=(
            jax.ShapeDtypeStruct((cap, size, size), bf16),
            jax.ShapeDtypeStruct(weights.shape, f32),
        ),
        in_specs=[smem] * 4 + [vmem] * 3 + [hbm] * 3,
        out_specs=(vmem, vmem),
        scratch_shapes=[
            pltpu.VMEM((blocks, half, size), bf16),
            pltpu.VMEM((blocks, half, size), bf16),
            pltpu.VMEM((cap, n, half, size), bf16),
            pltpu.VMEM(left_codes.shape, bf16),
            pltpu.VMEM(right_codes.shape, bf16),
            pltpu.VMEM(weights.shape, f32),
            pltpu.VMEM((size, width), bf16),
            pltpu.VMEM((cap, size, width), bf16),
            pltpu.VMEM((n * cap, rows, width), bf16),
            pltpu.VMEM((cap, 8, 128), f32),
            pltpu.VMEM((cap, 8, 128), f32),
            pltpu.VMEM((8, 128), f32),
            pltpu.VMEM((n, 8, 128), f32),
            dma((3,)), dma, dma, dma((cap,)),
            dma((cap, n)), dma((cap, n)), dma((cap, n)), dma((cap, n)),
            dma((cap, n)), dma((cap, n)), dma((cap,)), dma((cap,)), dma((n,)), dma((n,)),
        ],
        compiler_params=pltpu.CompilerParams(collective_id=0, has_side_effects=True),
    )(
        source, slot_of, owners, slot_of - owners * cap,
        grad_parts[0], left_scales, right_scales, left_codes, right_codes, weights,
    )

    first_row = replica * width
    rows_mine = lax.dynamic_slice_in_dim(whole_grad, first_row, width, 1)
    cols_mine = lax.dynamic_slice_in_dim(whole_grad, first_row, width, 2)
    gram_left = jnp.einsum("srk,sck->src", rows_mine, whole_grad, preferred_element_type=jnp.float32)
    gram_right = jnp.einsum("skr,skc->src", cols_mine, whole_grad, preferred_element_type=jnp.float32)
    left_new = stat_decay * left_stat + (1.0 - stat_decay) * gram_left
    right_new = stat_decay * right_stat + (1.0 - stat_decay) * gram_right
    return (new_weights, left_new, right_new)


def route_rows(summed, picker, owner_count, capacity):
    blocks = summed.shape[0]
    flat = summed.reshape(blocks, -1)
    placed = jnp.einsum("bj,bx->jx", picker, flat, preferred_element_type=jnp.float32).astype(
        jnp.bfloat16
    )
    return placed.reshape(owner_count, capacity, summed.shape[1], summed.shape[2])


def local(
    grad_parts, weights, left_stat, right_stat, left_codes, right_codes,
    left_scales, right_scales, owners,
):
    if kernels_fit(weights.shape[1], left_stat.shape[1], left_stat.shape[0]):
        return fast(
            grad_parts, weights, left_stat, right_stat, left_codes, right_codes,
            left_scales, right_scales, owners,
        )
    owner_count = lax.axis_size("fsdp")
    replica = lax.axis_index("dp")
    capacity = left_stat.shape[0]
    piece_width = left_stat.shape[1]
    block_width = left_codes.shape[1]
    slot_of = slot_table(owners, capacity)
    slot_ids = jnp.arange(owner_count * capacity, dtype=jnp.int32)
    picker = (slot_of[:, None] == slot_ids[None, :]).astype(jnp.bfloat16)
    partial_value = grad_parts[0].astype(jnp.float32)
    summed = lax.psum_scatter(
        partial_value.astype(jnp.bfloat16), "dp", scatter_dimension=2, tiled=True
    )
    routed = route_rows(summed, picker, owner_count, capacity)
    arrived = lax.all_to_all(routed, "fsdp", split_axis=0, concat_axis=2, tiled=True)
    column_part = arrived.reshape(capacity, block_width, piece_width)
    whole_grad = lax.all_gather(column_part, "dp", axis=2, tiled=True)
    first_row = replica * piece_width
    rows_mine = lax.dynamic_slice_in_dim(whole_grad, first_row, piece_width, 1)
    cols_mine = lax.dynamic_slice_in_dim(whole_grad, first_row, piece_width, 2)
    gram_left = jnp.einsum(
        "srk,sck->src", rows_mine, whole_grad, preferred_element_type=jnp.float32
    )
    gram_right = jnp.einsum(
        "skr,skc->src", cols_mine, whole_grad, preferred_element_type=jnp.float32
    )
    left_new = stat_decay * left_stat + (1.0 - stat_decay) * gram_left
    right_new = stat_decay * right_stat + (1.0 - stat_decay) * gram_right
    left_factor = (left_codes.astype(jnp.float32) * left_scales[:, :, None]).astype(jnp.bfloat16)
    right_factor = (right_codes.astype(jnp.float32) * right_scales[:, :, None]).astype(jnp.bfloat16)
    mixed = jnp.einsum(
        "sik,sck->sic", whole_grad, right_factor, preferred_element_type=jnp.float32
    ).astype(jnp.bfloat16)
    precond = jnp.einsum("sik,skc->sic", left_factor, mixed, preferred_element_type=jnp.float32)
    part_squares = jnp.sum(precond * precond, axis=(1, 2))
    total_squares = lax.psum(part_squares, "dp")
    grad_squares = jnp.sum(jnp.square(whole_grad.astype(jnp.float32)), axis=(1, 2))
    graft_ratio = jnp.sqrt(grad_squares) * lax.rsqrt(total_squares + epsilon)
    update = step_size * graft_ratio[:, None, None] * precond
    returned = lax.all_to_all(update, "fsdp", split_axis=1, concat_axis=0, tiled=True)
    my_update = jnp.take(returned, slot_of, axis=0)
    new_weights = weights - my_update
    return (new_weights, left_new, right_new)


def solution(mesh):
    return jax.shard_map(
        local,
        mesh=mesh,
        in_specs=(
            P("dp", None, "fsdp", None),
            P(None, "fsdp", "dp"),
            P("fsdp", "dp", None),
            P("fsdp", "dp", None),
            P("fsdp", None, None),
            P("fsdp", "dp", None),
            P("fsdp", None),
            P("fsdp", "dp"),
            P(),
        ),
        out_specs=(P(None, "fsdp", "dp"), P("fsdp", "dp", None), P("fsdp", "dp", None)),
        check_vma=False,
    )
```

```python
import functools

import jax
import jax.numpy as jnp
from jax import lax
from jax.experimental import pallas as pl
from jax.experimental.pallas import tpu as pltpu
from jax.sharding import PartitionSpec as P

stat_decay = 0.95
step_size = 0.5
epsilon = 1e-06
MESH = pl.DeviceIdType.MESH


def slot_table(owners, capacity):
    count = owners.shape[0]
    index = jnp.arange(count, dtype=jnp.int32)
    earlier = (owners[:, None] == owners[None, :]) & (index[None, :] < index[:, None])
    rank = jnp.sum(earlier.astype(jnp.int32), axis=1)
    return owners * capacity + rank


def greet(n, me, core):
    barrier = pltpu.get_barrier_semaphore()

    @pl.loop(1, n)
    def _(k):
        peer = lax.rem(me + k, n)
        pl.semaphore_signal(barrier, inc=1, device_id=(peer, core), device_id_type=MESH)

    pl.semaphore_signal(barrier, inc=1, device_id=(me, 1 - core), device_id_type=MESH)


def fill_tables(n, cap, blocks, owner_ref, slot_ref, rank_ref, source_ref):
    slots = []
    for b in range(blocks):
        rank = jnp.int32(0)
        for c in range(b):
            rank = rank + jnp.where(owner_ref[c] == owner_ref[b], 1, 0).astype(jnp.int32)
        rank = lax.min(rank, jnp.int32(cap - 1))
        slots.append(owner_ref[b] * cap + rank)
        slot_ref[b] = slots[b]
        rank_ref[b] = rank

    @pl.loop(0, n * cap)
    def _(j):
        code = jnp.int32(-1)
        for b in range(blocks):
            code = jnp.where(slots[b] == j, jnp.int32(b), code)
        source_ref[j] = code


def step_kernel(
    n, cap, owner_ref, grad_ref, left_scale_ref, right_scale_ref,
    left_hbm, right_hbm, weights_hbm, left_stat_hbm, right_stat_hbm,
    out_ref, left_new_ref, right_new_ref,
    slot_ref, rank_ref, source_ref, whole, left_stat_ref, right_stat_ref, theirs, summed, stage, left_ref, right_ref, weights_ref, mixed_ref, pre_ref, landed,
    squares, other_squares, graft, grafts,
    load_sem, store_sem, swap_send, swap_recv, own_sem, out_send, out_recv, fwd_send, fwd_recv,
    back_send, back_recv, sq_send, sq_recv, tiny_send, tiny_recv,
):
    me = lax.axis_index("fsdp")
    core = lax.axis_index("dp")
    blocks, rows, size = grad_ref.shape
    half = rows // 2
    loads = [
        pltpu.make_async_copy(right_hbm, right_ref, load_sem.at[0]),
        pltpu.make_async_copy(left_hbm, left_ref, load_sem.at[1]),
        pltpu.make_async_copy(weights_hbm, weights_ref, load_sem.at[2]),
        pltpu.make_async_copy(left_stat_hbm, left_stat_ref, load_sem.at[3]),
        pltpu.make_async_copy(right_stat_hbm, right_stat_ref, load_sem.at[4]),
    ]
    greet(n, me, core)
    for load in loads:
        load.start()
    fill_tables(n, cap, blocks, owner_ref, slot_ref, rank_ref, source_ref)
    pl.semaphore_wait(pltpu.get_barrier_semaphore(), n)

    other_rows = pl.ds(pl.multiple_of((1 - core) * half, half), half)
    my_rows = pl.ds(pl.multiple_of(core * half, half), half)
    swap = pltpu.make_async_remote_copy(
        src_ref=grad_ref.at[:, other_rows, :], dst_ref=theirs,
        send_sem=swap_send, recv_sem=swap_recv,
        device_id=(me, 1 - core), device_id_type=MESH,
    )
    swap.start()
    swap.wait()
    summed[...] = (
        grad_ref[:, my_rows, :].astype(jnp.float32) + theirs[...].astype(jnp.float32)
    ).astype(jnp.bfloat16)

    def landing(slot, device, its_core):
        start = pl.multiple_of(device * rows + its_core * half, half)
        return whole.at[slot, pl.ds(start, half), :]

    def outward(slot, k, peer, origin):
        return pltpu.make_async_remote_copy(
            src_ref=stage.at[slot, peer], dst_ref=landing(slot, origin, core),
            send_sem=out_send.at[slot, k], recv_sem=out_recv.at[slot, k],
            device_id=(peer, core), device_id_type=MESH,
        )

    def forward(slot, k, its_core):
        peer = lax.rem(me - k + n, n)
        return pltpu.make_async_remote_copy(
            src_ref=landing(slot, peer, its_core), dst_ref=landing(slot, peer, its_core),
            send_sem=fwd_send.at[slot, k], recv_sem=fwd_recv.at[slot, k],
            device_id=(me, 1 - core), device_id_type=MESH,
        )

    def back(slot, k, peer, origin):
        return pltpu.make_async_remote_copy(
            src_ref=pre_ref.at[slot, pl.ds(pl.multiple_of(peer * rows, rows), rows), :],
            dst_ref=landed.at[origin * cap + slot],
            send_sem=back_send.at[slot, k], recv_sem=back_recv.at[slot, k],
            device_id=(peer, core), device_id_type=MESH,
        )

    def tiny(k, peer, origin):
        return pltpu.make_async_remote_copy(
            src_ref=graft, dst_ref=grafts.at[origin],
            send_sem=tiny_send.at[k], recv_sem=tiny_recv.at[k],
            device_id=(peer, core), device_id_type=MESH,
        )

    def swap_squares(slot):
        return pltpu.make_async_remote_copy(
            src_ref=squares.at[slot], dst_ref=other_squares.at[slot],
            send_sem=sq_send.at[slot], recv_sem=sq_recv.at[slot],
            device_id=(me, 1 - core), device_id_type=MESH,
        )

    def own(slot):
        return pltpu.make_async_copy(stage.at[slot, me], landing(slot, me, core), own_sem.at[slot])

    def store(side, slot):
        kept = (left_stat_ref, right_stat_ref)[side]
        result = (left_new_ref, right_new_ref)[side]
        return pltpu.make_async_copy(kept.at[slot], result.at[slot], store_sem.at[side, slot])

    def nth(i):
        return i + 1

    @pl.loop(0, cap)
    def _(slot):
        @pl.loop(0, n)
        def _(peer):
            code = source_ref[peer * cap + slot]
            piece = summed[lax.max(code, 0)].astype(jnp.float32)
            keep = jnp.where(code >= 0, 1.0, 0.0).astype(jnp.float32)
            stage[slot, peer] = (piece * keep).astype(jnp.bfloat16)

        own(slot).start()

        @pl.loop(0, n - 1)
        def _(i):
            k = nth(i)
            outward(slot, k, lax.rem(me + k, n), me).start()

    @pl.loop(0, cap)
    def _(slot):
        own(slot).wait()
        forward(slot, 0, core).start()

    for load in loads[:2]:
        load.wait()

    def scaled(codes, scale_row):
        count = codes.shape[0]
        column = jnp.transpose(jnp.broadcast_to(scale_row, (8, count)))[:, 0:1]
        return (codes.astype(jnp.float32) * column).astype(jnp.bfloat16)

    for slot in range(cap):
        right_ref[slot] = scaled(right_ref[slot], right_scale_ref[pl.ds(slot, 1), :])
        left_ref[slot] = scaled(left_ref[slot], left_scale_ref[pl.ds(slot, 1), :])

    @pl.loop(0, cap)
    def _(slot):
        @pl.loop(0, n - 1)
        def _(i):
            k = nth(i)
            outward(slot, k, me, lax.rem(me - k + n, n)).wait_recv()
            forward(slot, k, core).start()

        @pl.loop(0, n)
        def _(k):
            forward(slot, k, 1 - core).wait_recv()

        mixed_ref[...] = lax.dot_general(
            whole[slot], right_ref[slot], (((1,), (1,)), ((), ())),
            preferred_element_type=jnp.float32,
        ).astype(jnp.bfloat16)
        pre = jnp.dot(left_ref[slot], mixed_ref[...], preferred_element_type=jnp.float32)
        pre_ref[slot] = pre.astype(jnp.bfloat16)
        squares[slot] = jnp.full(squares.shape[1:], jnp.sum(pre * pre), jnp.float32)

        @pl.loop(0, n - 1)
        def _(i):
            k = nth(i)
            back(slot, k, lax.rem(me + k, n), me).start()

        swap_squares(slot).start()
        landed[me * cap + slot] = pre_ref[slot, pl.ds(pl.multiple_of(me * rows, rows), rows), :]

    line = lax.broadcasted_iota(jnp.int32, graft.shape, 0)
    factor = jnp.zeros(graft.shape, jnp.float32)
    for slot in range(cap):
        energy = jnp.sum(jnp.square(whole[slot].astype(jnp.float32)))
        swap_squares(slot).wait()
        total = squares[slot] + other_squares[slot]
        ratio = step_size * jnp.sqrt(jnp.full(graft.shape, energy, jnp.float32))
        factor = jnp.where(line == slot, ratio * lax.rsqrt(total + epsilon), factor)
    graft[...] = factor
    grafts[me] = factor

    @pl.loop(0, n - 1)
    def _(i):
        k = nth(i)
        tiny(k, lax.rem(me + k, n), me).start()

    for load in loads[2:]:
        load.wait()
    width = left_stat_ref.shape[1]
    mine = pl.ds(pl.multiple_of(core * width, width), width)

    @pl.loop(0, cap)
    def _(slot):
        gram = lax.dot_general(
            whole[slot, mine, :], whole[slot], (((1,), (1,)), ((), ())),
            preferred_element_type=jnp.float32,
        )
        left_stat_ref[slot] = stat_decay * left_stat_ref[slot] + (1.0 - stat_decay) * gram
        store(0, slot).start()
        gram = lax.dot_general(
            whole[slot, :, mine], whole[slot], (((0,), (0,)), ((), ())),
            preferred_element_type=jnp.float32,
        )
        right_stat_ref[slot] = stat_decay * right_stat_ref[slot] + (1.0 - stat_decay) * gram
        store(1, slot).start()

    @pl.loop(0, cap)
    def _(slot):
        @pl.loop(1, n)
        def _(k):
            back(slot, k, me, lax.rem(me - k + n, n)).wait_recv()

    @pl.loop(1, n)
    def _(k):
        tiny(k, me, lax.rem(me - k + n, n)).wait_recv()

    @pl.loop(0, blocks)
    def _(b):
        amount = grafts[owner_ref[b], pl.ds(rank_ref[b], 1), :]
        update = landed[slot_ref[b]].astype(jnp.float32)
        for start in range(0, update.shape[1], 128):
            part = slice(start, start + 128)
            out_ref[b, :, part] = weights_ref[b, :, part] - amount * update[:, part]

    @pl.loop(0, cap)
    def _(slot):
        @pl.loop(1, n)
        def _(k):
            peer = lax.rem(me + k, n)
            outward(slot, k, peer, me).wait_send()
            back(slot, k, peer, me).wait_send()

        @pl.loop(0, n)
        def _(k):
            forward(slot, k, core).wait_send()

        store(0, slot).wait()
        store(1, slot).wait()

    @pl.loop(1, n)
    def _(k):
        tiny(k, lax.rem(me + k, n), me).wait_send()


def kernels_fit(rows, width, capacity):
    return lax.axis_size("dp") == 2 and rows % 32 == 0 and width % 128 == 0 and capacity <= 8


def fast(
    grad_parts, weights, left_stat, right_stat, left_codes, right_codes,
    left_scales, right_scales, owners,
):
    n = lax.axis_size("fsdp")
    cap, width, size = left_stat.shape
    blocks, rows = weights.shape[:2]
    half = rows // 2
    vmem = pl.BlockSpec(memory_space=pltpu.VMEM)
    smem = pl.BlockSpec(memory_space=pltpu.SMEM)
    hbm = pl.BlockSpec(memory_space=pl.ANY)
    dma = pltpu.SemaphoreType.DMA
    bf16, f32 = jnp.bfloat16, jnp.float32
    return pl.pallas_call(
        functools.partial(step_kernel, n, cap),
        out_shape=(
            jax.ShapeDtypeStruct(weights.shape, f32),
            jax.ShapeDtypeStruct(left_stat.shape, f32),
            jax.ShapeDtypeStruct(right_stat.shape, f32),
        ),
        in_specs=[smem] + [vmem] * 3 + [hbm] * 5,
        out_specs=(vmem, hbm, hbm),
        scratch_shapes=[
            pltpu.SMEM((blocks,), jnp.int32),
            pltpu.SMEM((blocks,), jnp.int32),
            pltpu.SMEM((n * cap,), jnp.int32),
            pltpu.VMEM((cap, size, size), bf16),
            pltpu.VMEM(left_stat.shape, f32),
            pltpu.VMEM(right_stat.shape, f32),
            pltpu.VMEM((blocks, half, size), bf16),
            pltpu.VMEM((blocks, half, size), bf16),
            pltpu.VMEM((cap, n, half, size), bf16),
            pltpu.VMEM(left_codes.shape, bf16),
            pltpu.VMEM(right_codes.shape, bf16),
            pltpu.VMEM(weights.shape, f32),
            pltpu.VMEM((size, width), bf16),
            pltpu.VMEM((cap, size, width), bf16),
            pltpu.VMEM((n * cap, rows, width), bf16),
            pltpu.VMEM((cap, 8, 128), f32),
            pltpu.VMEM((cap, 8, 128), f32),
            pltpu.VMEM((8, 128), f32),
            pltpu.VMEM((n, 8, 128), f32),
            dma((5,)), dma((2, cap)), dma, dma, dma((cap,)),
            dma((cap, n)), dma((cap, n)), dma((cap, n)), dma((cap, n)),
            dma((cap, n)), dma((cap, n)), dma((cap,)), dma((cap,)), dma((n,)), dma((n,)),
        ],
        compiler_params=pltpu.CompilerParams(collective_id=0, has_side_effects=True),
    )(
        owners, grad_parts[0], left_scales, right_scales,
        left_codes, right_codes, weights, left_stat, right_stat,
    )


def route_rows(summed, picker, owner_count, capacity):
    blocks = summed.shape[0]
    flat = summed.reshape(blocks, -1)
    placed = jnp.einsum("bj,bx->jx", picker, flat, preferred_element_type=jnp.float32).astype(
        jnp.bfloat16
    )
    return placed.reshape(owner_count, capacity, summed.shape[1], summed.shape[2])


def local(
    grad_parts, weights, left_stat, right_stat, left_codes, right_codes,
    left_scales, right_scales, owners,
):
    if kernels_fit(weights.shape[1], left_stat.shape[1], left_stat.shape[0]):
        return fast(
            grad_parts, weights, left_stat, right_stat, left_codes, right_codes,
            left_scales, right_scales, owners,
        )
    owner_count = lax.axis_size("fsdp")
    replica = lax.axis_index("dp")
    capacity = left_stat.shape[0]
    piece_width = left_stat.shape[1]
    block_width = left_codes.shape[1]
    slot_of = slot_table(owners, capacity)
    slot_ids = jnp.arange(owner_count * capacity, dtype=jnp.int32)
    picker = (slot_of[:, None] == slot_ids[None, :]).astype(jnp.bfloat16)
    partial_value = grad_parts[0].astype(jnp.float32)
    summed = lax.psum_scatter(
        partial_value.astype(jnp.bfloat16), "dp", scatter_dimension=2, tiled=True
    )
    routed = route_rows(summed, picker, owner_count, capacity)
    arrived = lax.all_to_all(routed, "fsdp", split_axis=0, concat_axis=2, tiled=True)
    column_part = arrived.reshape(capacity, block_width, piece_width)
    whole_grad = lax.all_gather(column_part, "dp", axis=2, tiled=True)
    first_row = replica * piece_width
    rows_mine = lax.dynamic_slice_in_dim(whole_grad, first_row, piece_width, 1)
    cols_mine = lax.dynamic_slice_in_dim(whole_grad, first_row, piece_width, 2)
    gram_left = jnp.einsum(
        "srk,sck->src", rows_mine, whole_grad, preferred_element_type=jnp.float32
    )
    gram_right = jnp.einsum(
        "skr,skc->src", cols_mine, whole_grad, preferred_element_type=jnp.float32
    )
    left_new = stat_decay * left_stat + (1.0 - stat_decay) * gram_left
    right_new = stat_decay * right_stat + (1.0 - stat_decay) * gram_right
    left_factor = (left_codes.astype(jnp.float32) * left_scales[:, :, None]).astype(jnp.bfloat16)
    right_factor = (right_codes.astype(jnp.float32) * right_scales[:, :, None]).astype(jnp.bfloat16)
    mixed = jnp.einsum(
        "sik,sck->sic", whole_grad, right_factor, preferred_element_type=jnp.float32
    ).astype(jnp.bfloat16)
    precond = jnp.einsum("sik,skc->sic", left_factor, mixed, preferred_element_type=jnp.float32)
    part_squares = jnp.sum(precond * precond, axis=(1, 2))
    total_squares = lax.psum(part_squares, "dp")
    grad_squares = jnp.sum(jnp.square(whole_grad.astype(jnp.float32)), axis=(1, 2))
    graft_ratio = jnp.sqrt(grad_squares) * lax.rsqrt(total_squares + epsilon)
    update = step_size * graft_ratio[:, None, None] * precond
    returned = lax.all_to_all(update, "fsdp", split_axis=1, concat_axis=0, tiled=True)
    my_update = jnp.take(returned, slot_of, axis=0)
    new_weights = weights - my_update
    return (new_weights, left_new, right_new)


def solution(mesh):
    return jax.shard_map(
        local,
        mesh=mesh,
        in_specs=(
            P("dp", None, "fsdp", None),
            P(None, "fsdp", "dp"),
            P("fsdp", "dp", None),
            P("fsdp", "dp", None),
            P("fsdp", None, None),
            P("fsdp", "dp", None),
            P("fsdp", None),
            P("fsdp", "dp"),
            P(),
        ),
        out_specs=(P(None, "fsdp", "dp"), P("fsdp", "dp", None), P("fsdp", "dp", None)),
        check_vma=False,
    )
```
